32 devices in a mesh: dp: 16 (over z, y, x), tensor: 2 (over core).
Axes of the slice: x: 2, y: 2, z: 4, core: 2. Of those that a mesh axis runs over, the one named last changes fastest.
Arguments:
- inputs: bfloat16 [11776, 1152], P(('dp', 'tensor')), may hold values from -140 to 140
- key_mask: int32 [16, 736], P('dp'), may hold values from 0 to 1, as said below
- norm_gain: float32 [2, 1152], replicated, may hold values from 0.5 to 1.5
- norm_bias: float32 [2, 1152], replicated, may hold values from -3 to 3
- w_qkv: bfloat16 [3, 1152, 1152], P(None, 'dp', 'tensor'), may hold values from -13 to 13
- qv_bias: float32 [2, 1152], P(None, 'tensor'), may hold values from -3 to 3
- w_out: bfloat16 [1152, 1152], P('tensor', 'dp'), may hold values from -3 to 3
- out_bias: float32 [1152], replicated, may hold values from -3 to 3
- w_up: bfloat16 [1152, 4304], P('dp', 'tensor'), may hold values from -0.1875 to 0.1875
- up_bias: float32 [4304], P('tensor'), may hold values from -3 to 3
- w_down: bfloat16 [4304, 1152], P('tensor', 'dp'), may hold values from -0.09375 to 0.09375
- down_bias: float32 [1152], replicated, may hold values from -3 to 3
- grad_out: bfloat16 [11776, 1152], P(('dp', 'tensor')), may hold values from -6 to 6
Outputs:
- outputs: float32 [11776, 1152], P(('dp', 'tensor'))
- grad_inputs: float32 [11776, 1152], P(('dp', 'tensor'))
- grad_norm_gain: float32 [2, 1152], replicated
- grad_norm_bias: float32 [2, 1152], replicated
- grad_w_qkv: float32 [3, 1152, 1152], P(None, 'dp', 'tensor')
- grad_qv_bias: float32 [2, 1152], P(None, 'tensor')
- grad_w_out: float32 [1152, 1152], P('tensor', 'dp')
- grad_out_bias: float32 [1152], replicated
- grad_w_up: float32 [1152, 4304], P('dp', 'tensor')
- grad_up_bias: float32 [4304], P('tensor')
- grad_w_down: float32 [4304, 1152], P('tensor', 'dp')
- grad_down_bias: float32 [1152], replicated
The draws below stay inside these ranges and needn't reach their ends.
Inputs may be any that keep to these rules, and one draw needn't show every extreme that they name: `key_mask`: each row holds exactly 729 ones, the rest zeros.
All inputs are finite; a program needn't handle non-finite values.
Results may differ from the reference program's by a relative error of at most 0.013.
The reference program's roundings to bfloat16 on the way count: a program that leaves them out, or rounds other values in their place, can miss the bound.
Values may be sent and summed in bfloat16 or wider, within the bound.
No kernel may reach another device: no remote copies, remote signals or barrier semaphores. Data moves between devices by JAX's collectives and lax.ppermute only.
A program may use at most 192 MiB of HBM per device.

```python
import jax
import jax.numpy as jnp
from jax import lax

D = 1152
FF = 4304
HEADS = 16
HEAD = 72
SEQ = 736
VALID = 729
IMGS = 1
NIMG = 16
TOKENS = 11776
N_DP = 16


def draw_inputs(key, part):
    base_draw = jnp.clip(jax.random.normal(jax.random.fold_in(key, 13), (TOKENS, D), jnp.float32), -4.0, 4.0)
    col_scale = jnp.exp(jax.random.uniform(jax.random.fold_in(key, 14), (1, D), jnp.float32, jnp.log(0.3), jnp.log(3.0)))
    row_scale = jnp.exp(jax.random.uniform(jax.random.fold_in(key, 15), (TOKENS, 1), jnp.float32, jnp.log(0.3), jnp.log(3.0)))
    owner = jax.random.permutation(jax.random.fold_in(key, 16), N_DP)
    group_ids = (jnp.arange(TOKENS) // (SEQ * IMGS))[:, None]
    block_ids = (jnp.arange(D) // (D // N_DP))[None, :]
    spiked = jnp.where(owner[group_ids] == block_ids, 3.0, 1.0)
    field = base_draw * col_scale * row_scale * spiked
    return field.astype(jnp.bfloat16)


def draw_w_qkv(key, part):
    base_draw = jnp.clip(jax.random.normal(jax.random.fold_in(key, 21), (3, D, D), jnp.float32), -4.0, 4.0) * D ** (-0.5)
    return base_draw.astype(jnp.bfloat16)


def draw_key_mask(key, part):
    image_keys = jax.random.split(jax.random.fold_in(key, 31), NIMG)

    def ranked(member):
        return jax.random.permutation(member, SEQ)
    ranks = jax.vmap(ranked)(image_keys)
    return (ranks >= SEQ - VALID).astype(jnp.int32)


def raised(values, stream_key, source, target, blocks, factor):
    owner, partner = [(jnp.arange(values.shape[position]) // (values.shape[position] // blocks)).reshape([-1 if axis == position else 1 for axis in range(values.ndim)]) for position in (source, target)]
    chosen = jax.random.permutation(stream_key, blocks)[partner]
    strong = (owner == chosen) | (owner == (partner + blocks // 2) % blocks)
    return jnp.where(strong, factor * values, values)


def steps_of(key, shape, cuts, smallest, top_value):
    gain, own = 1.0, jax.random.fold_in(key, 6)
    for axis_at, parts in cuts:
        steps = jnp.exp(jax.random.uniform(jax.random.fold_in(own, axis_at), (parts,), jnp.float32, smallest / len(cuts), top_value / len(cuts)))
        gain = gain * jnp.repeat(steps, shape[axis_at] // parts).reshape([-1 if axis == axis_at else 1 for axis in range(len(shape))])
    return gain


def scatter_about(rng, shape, scale, reach, pieces=(), dtype=jnp.bfloat16):
    loudness = steps_of(rng, shape, pieces, -0.22, 0.18) if pieces else 1.0
    entries = jax.random.normal(rng, shape, jnp.float32) * scale * loudness
    return jnp.minimum(jnp.maximum(entries, -reach), reach).astype(dtype)


def heavy_noise(own_key, dims, width, bound, cuts, heavy, kind=jnp.bfloat16):
    entries = width * jax.random.normal(own_key, dims, jnp.float32)
    if cuts:
        entries = entries * steps_of(own_key, dims, cuts, -0.22, 0.18)
    return jnp.clip(raised(entries, jax.random.fold_in(own_key, 3), *heavy), -bound, bound).astype(kind)


def setup_inputs(seed: int = 0) -> dict:
    keys = jax.random.split(jax.random.key(seed), 14)
    return {
        "inputs": draw_inputs(jax.random.fold_in(keys[13], 71), 0),
        "key_mask": draw_key_mask(jax.random.fold_in(keys[13], 71), 0),
        "norm_gain": jnp.clip(jax.random.uniform(keys[2], (2, D), jnp.float32, 0.5, 1.5), 0.5, 1.5),
        "norm_bias": scatter_about(keys[3], (2, D), 0.5, 3.0, (), jnp.float32),
        "w_qkv": draw_w_qkv(jax.random.fold_in(keys[13], 71), 0),
        "qv_bias": scatter_about(keys[5], (2, D), 0.5, 3.0, ((1, 2),), jnp.float32),
        "w_out": scatter_about(keys[6], (D, D), (max(3 * D // SEQ, 1)) ** -0.5, 3.0, ((0, 2), (1, 16))),
        "out_bias": scatter_about(keys[7], (D,), 0.5, 3.0, (), jnp.float32),
        "w_up": scatter_about(keys[8], (D, FF), D ** -0.5, 0.1875, ((0, 16), (1, 2))),
        "up_bias": scatter_about(keys[9], (FF,), 0.5, 3.0, ((0, 2),), jnp.float32),
        "w_down": scatter_about(keys[10], (FF, D), FF ** -0.5, 0.09375, ((0, 2), (1, 16))),
        "down_bias": scatter_about(keys[11], (D,), 0.5, 3.0, (), jnp.float32),
        "grad_out": heavy_noise(keys[12], (TOKENS, D), 1.0, 6.0, ((0, 32),), (0, 1, 32, 2.75)),
    }


@jax.custom_vjp
def low(v):
    return lax.optimization_barrier(v.astype(jnp.bfloat16)).astype(jnp.float32)

@jax.custom_vjp
def low_back(v):
    return v

def low_keep(v):
    return (low(v), None)

def low_pass(kept, grad):
    return (grad,)

def back_keep(v):
    return (v, None)

def back_low(kept, grad):
    return (low(grad),)
low.defvjp(low_keep, low_pass)
low_back.defvjp(back_keep, back_low)
PRECISE = lax.Precision.HIGHEST
EPSILON = 1e-06

def norm_layer(input_rows, gain_vec, shift_vec):
    row_mean = lax.optimization_barrier(jnp.mean(input_rows, axis=-1, keepdims=True))
    centered = input_rows - row_mean
    row_var = lax.optimization_barrier(jnp.mean(centered * centered, axis=-1, keepdims=True))
    return centered * lax.rsqrt(row_var + EPSILON) * gain_vec + shift_vec

def attend_image(queries, key_rows, values, valid_keys):
    raw_scores = low_back(jnp.einsum('qhd,khd->hqk', queries, key_rows, precision=PRECISE))
    logits = jnp.where(valid_keys[None, None, :] > 0, raw_scores * HEAD ** (-0.5), -1e+30)
    row_top = lax.optimization_barrier(jnp.max(logits, axis=-1, keepdims=True))
    exp_scores = jnp.exp(logits - row_top)
    softmax_w = exp_scores / lax.optimization_barrier(jnp.sum(exp_scores, axis=-1, keepdims=True))
    attn_mixed = jnp.einsum('hqk,khd->qhd', low(softmax_w), values, precision=PRECISE)
    return low(low_back(attn_mixed))

def layer(inputs, norm_gain, norm_bias, w_qkv, qv_bias, w_out, out_bias, w_up, up_bias, w_down, down_bias, key_mask):
    normed_one = low(norm_layer(inputs, norm_gain[0], norm_bias[0]))
    projected = jnp.einsum('td,kde->kte', normed_one, w_qkv, precision=PRECISE)
    queries = low(low_back(projected[0] + qv_bias[0]))
    key_rows = low(low_back(projected[1]))
    values = low(low_back(projected[2] + qv_bias[1]))
    head_shape = (key_mask.shape[0], SEQ, HEADS, HEAD)
    checked = jax.checkpoint(attend_image)

    def one_image(member):
        return checked(member[0], member[1], member[2], member[3])
    attn_mixed = lax.map(one_image, (queries.reshape(head_shape), key_rows.reshape(head_shape), values.reshape(head_shape), key_mask))
    attn_mixed = attn_mixed.reshape(inputs.shape[0], D)
    branch = low_back(jnp.dot(attn_mixed, w_out, precision=PRECISE) + out_bias)
    middle = inputs + branch
    normed_two = low(norm_layer(middle, norm_gain[1], norm_bias[1]))
    pre_act = low_back(jnp.dot(normed_two, w_up, precision=PRECISE) + up_bias)
    hidden = low(jax.nn.gelu(pre_act, approximate=True))
    return middle + jnp.dot(hidden, w_down, precision=PRECISE) + down_bias

def reference(inputs, key_mask, norm_gain, norm_bias, w_qkv, qv_bias, w_out, out_bias, w_up, up_bias, w_down, down_bias, grad_out):
    params = (inputs.astype(jnp.float32), norm_gain, norm_bias, w_qkv.astype(jnp.float32), qv_bias, w_out.astype(jnp.float32), out_bias, w_up.astype(jnp.float32), up_bias, w_down.astype(jnp.float32), down_bias)

    def forward(*arguments):
        return layer(*arguments, key_mask)
    result, pullback = jax.vjp(forward, *params)
    gradients = pullback(grad_out.astype(jnp.float32))
    return (result, gradients[0], gradients[1], gradients[2], gradients[3], gradients[4], gradients[5], gradients[6], gradients[7], gradients[8], gradients[9], gradients[10])
```

```python
import jax
import jax.numpy as jnp
from jax import lax
from jax.sharding import PartitionSpec as P

HEAD = 72
EPSILON = 1e-06
F32 = jnp.float32
BF16 = jnp.bfloat16
F16 = jnp.float16
TAIL = 8


def norm_layer(input_rows, gain_vec, shift_vec):
    row_mean = jnp.mean(input_rows, axis=-1, keepdims=True)
    centered = input_rows - row_mean
    row_var = jnp.mean(centered * centered, axis=-1, keepdims=True)
    return centered * lax.rsqrt(row_var + EPSILON) * gain_vec + shift_vec


def gelu_tanh(pre_values):
    return jax.nn.gelu(pre_values, approximate=True)


def masked_logits(queries, key_rows, valid_keys, score_scale):
    raw_scores = jnp.einsum("qhd,khd->hqk", queries, key_rows, preferred_element_type=F32)
    return jnp.where(valid_keys[None, None, :] > 0, raw_scores * score_scale, -1e30)


def attend_forward(queries, key_rows, values, valid_keys, score_scale):
    logits = masked_logits(queries, key_rows, valid_keys, score_scale)
    row_top = jnp.max(logits, axis=-1, keepdims=True)
    exp_scores = jnp.exp(logits - row_top)
    exp_total = jnp.sum(exp_scores, axis=-1, keepdims=True)
    softmax_w = exp_scores / exp_total
    attn_mixed = jnp.einsum("hqk,khd->qhd", softmax_w.astype(BF16), values, preferred_element_type=F32)
    return (attn_mixed.astype(BF16), (row_top + jnp.log(exp_total))[..., 0])


def attend_backward(queries, key_rows, values, valid_keys, score_scale, log_norm, grad_mixed):
    logits = masked_logits(queries, key_rows, valid_keys, score_scale)
    softmax_w = jnp.exp(logits - log_norm[..., None])
    grad_probs = jnp.einsum("qhd,khd->hqk", grad_mixed, values, preferred_element_type=F32)
    row_inner = jnp.sum(softmax_w * grad_probs, axis=-1, keepdims=True)
    grad_raw = (softmax_w * (grad_probs - row_inner) * score_scale).astype(BF16)
    grad_queries = jnp.einsum("hqk,khd->qhd", grad_raw, key_rows, preferred_element_type=F32)
    grad_keys = jnp.einsum("hqk,qhd->khd", grad_raw, queries, preferred_element_type=F32)
    grad_values = jnp.einsum("hqk,qhd->khd", softmax_w.astype(BF16), grad_mixed, preferred_element_type=F32)
    return (grad_queries, grad_keys, grad_values)


def nt(a, b):
    return lax.dot_general(a, b, (((1,), (1,)), ((), ())), preferred_element_type=F32)


def tn(a, b):
    return lax.dot_general(a, b, (((0,), (0,)), ((), ())), preferred_element_type=F32)


def nn(a, b):
    return jnp.dot(a, b, preferred_element_type=F32)


class Ring:
    def __init__(self):
        self.size = lax.axis_size("dp")
        self.outer = self.size // 4
        self.index = lax.axis_index("dp")
        self.xb = self.index & 1
        self.yb = (self.index >> 1) & 1
        self.bits = []
        bit = 4
        while bit < self.size:
            self.bits.append(bit)
            bit *= 2

    def swap(self, value, bit):
        return lax.ppermute(value, "dp", [(i, i ^ bit) for i in range(self.size)])

    def has(self, bit):
        return (self.index & bit) != 0

    def gather(self, piece):
        rows, cols = piece.shape
        n = self.outer
        held = piece[None]
        for bit in reversed(self.bits):
            other = self.swap(held, bit)
            mine = self.has(bit)
            low, high = jnp.where(mine, other, held), jnp.where(mine, held, other)
            held = jnp.stack([low, high], axis=1).reshape(2 * held.shape[0], rows, cols)
        half = n // 2
        from_x = self.swap(held, 1)
        from_y = self.swap(held, 2)
        far_a = self.swap(from_x[:half], 2)
        far_b = self.swap(from_y[half:], 1)
        x, y = self.xb, self.yb
        whole = jnp.zeros((n, 2, 2, rows, cols), piece.dtype)
        for part, start in (
            (held, (0, y, x)),
            (from_x, (0, y, 1 - x)),
            (from_y, (0, 1 - y, x)),
            (far_a, (0, 1 - y, 1 - x)),
            (far_b, (half, 1 - y, 1 - x)),
        ):
            whole = lax.dynamic_update_slice(whole, part[:, None, None], tuple(jnp.int32(s) for s in start) + (jnp.int32(0),) * 2)
        return whole.reshape(n * 4 * rows, cols)

    def send(self, part, power, bit):
        n, rows, cols = part.shape
        tail = jnp.broadcast_to(power.astype(F16), (TAIL, cols))
        got = self.swap(jnp.concatenate([part.reshape(n * rows, cols), tail], axis=0), bit)
        got_power = got[n * rows, 0].astype(F32)
        return got[: n * rows].reshape(n, rows, cols).astype(F32) * jnp.exp2(got_power), got_power

    def reduce(self, grads, power):
        n = self.outer
        half = n // 2
        rows, cols = grads.shape[0] // self.size, grads.shape[1]
        grid = grads.reshape(n, 2, 2, rows, cols)
        x, y = self.xb, self.yb

        def quadrant(yy, xx, first=0, count=n):
            start = (jnp.int32(first), jnp.int32(yy), jnp.int32(xx), jnp.int32(0), jnp.int32(0))
            return lax.dynamic_slice(grid, start, (count, 1, 1, rows, cols)).reshape(count, rows, cols)

        scale = jnp.exp2(power)
        got_a, power_a = self.send(quadrant(1 - y, 1 - x, 0, half), power, 1)
        got_b, power_b = self.send(quadrant(1 - y, 1 - x, half, half), power, 2)
        power_y = jnp.maximum(power, power_a) + 1
        power_x = jnp.maximum(power, power_b) + 1
        near_y = quadrant(1 - y, x).astype(F32) * scale
        near_x = quadrant(y, 1 - x).astype(F32) * scale
        near_y = jnp.concatenate([near_y[:half] + got_a, near_y[half:]], axis=0)
        near_x = jnp.concatenate([near_x[:half], near_x[half:] + got_b], axis=0)
        got_x, power_gx = self.send((near_x * jnp.exp2(-power_x)).astype(F16), power_x, 1)
        got_y, power_gy = self.send((near_y * jnp.exp2(-power_y)).astype(F16), power_y, 2)
        held = quadrant(y, x).astype(F32) * scale + got_x + got_y
        power = jnp.maximum(jnp.maximum(power, power_gx), power_gy) + 2
        for bit in self.bits:
            mine = self.has(bit)
            pair = held.reshape(held.shape[0] // 2, 2, rows, cols)
            keep = jnp.where(mine, pair[:, 1], pair[:, 0])
            give = jnp.where(mine, pair[:, 0], pair[:, 1])
            got, got_power = self.send((give * jnp.exp2(-power)).astype(F16), power, bit)
            held = keep + got
            power = jnp.maximum(power, got_power) + 1
        return held.reshape(rows, cols)

    def total(self, values):
        bit = 1
        while bit < self.size:
            values = values + self.swap(values, bit)
            bit *= 2
        return values


def norm_of(value):
    wide = value.astype(F32)
    return jnp.sqrt(jnp.sum(wide * wide))


def power_for(a, b):
    bound = jnp.maximum(norm_of(a) * norm_of(b), 1e-30)
    return jnp.ceil(jnp.log2(bound)) - 14


def other_core(value):
    return lax.ppermute(value, "tensor", [(0, 1), (1, 0)])


def both(value):
    return jnp.concatenate([value, other_core(value)], axis=0)


def body(
    inputs,
    key_mask,
    norm_gain,
    norm_bias,
    w_qkv,
    qv_bias,
    w_out,
    out_bias,
    w_up,
    up_bias,
    w_down,
    down_bias,
    grad_out,
):
    ring = Ring()
    width = inputs.shape[1]
    images, seq_len = key_mask.shape
    half_width = w_qkv.shape[2]
    local_heads = half_width // HEAD
    score_scale = HEAD ** (-0.5)
    own = inputs.shape[0]
    all_rows = images * seq_len
    core = lax.axis_index("tensor")

    piece_one = jnp.concatenate([w_qkv[0], w_qkv[1], w_qkv[2], w_out.T], axis=1)
    inputs_all = both(inputs)
    grad_all = both(grad_out)
    weights_one = ring.gather(piece_one)
    up_full = ring.gather(w_up)
    down_t = ring.gather(w_down.T)
    qkv_full = weights_one[:, : 3 * half_width]
    out_t = weights_one[:, 3 * half_width :]

    mask = key_mask.reshape(images * seq_len)
    mask = jnp.where(core == 0, mask, jnp.concatenate([mask[own:], mask[:own]])).reshape(images, seq_len)

    inputs_wide = inputs.astype(F32)
    normed_one = norm_layer(inputs_all.astype(F32), norm_gain[0], norm_bias[0]).astype(BF16)
    projected = nn(normed_one, qkv_full)
    queries = (projected[:, :half_width] + qv_bias[0]).astype(BF16)
    key_rows = projected[:, half_width : 2 * half_width].astype(BF16)
    values = (projected[:, 2 * half_width :] + qv_bias[1]).astype(BF16)
    head_shape = (seq_len, local_heads, HEAD)
    stacked = (queries.reshape(head_shape), key_rows.reshape(head_shape), values.reshape(head_shape), mask[0])
    attn_mixed, log_norm = attend_forward(*stacked, score_scale)
    attn_mixed = attn_mixed.reshape(all_rows, half_width)
    attn_part = nt(attn_mixed, out_t)
    middle = inputs_wide + (attn_part[:own] + other_core(attn_part[own:]) + out_bias)
    normed_two = norm_layer(middle, norm_gain[1], norm_bias[1]).astype(BF16)
    normed_two_all = both(normed_two)
    pre_act = nn(normed_two_all, up_full) + up_bias
    hidden = gelu_tanh(pre_act).astype(BF16)

    down_power = power_for(grad_all, hidden)
    grad_down = (tn(grad_all, hidden) * jnp.exp2(-down_power)).astype(F16)
    grad_down_t = ring.reduce(grad_down, down_power)

    grad_hidden = nn(grad_all, down_t)
    grad_pre = jax.vjp(gelu_tanh, pre_act)[1](grad_hidden)[0].astype(BF16)
    grad_two_part = nt(grad_pre, up_full)
    grad_normed_two = grad_two_part[:own] + other_core(grad_two_part[own:].astype(BF16)).astype(F32)
    middle_pull = jax.vjp(norm_layer, middle, norm_gain[1], norm_bias[1])[1]
    grad_middle_part, grad_gain_two, grad_shift_two = middle_pull(grad_normed_two)
    grad_middle = grad_out.astype(F32) + grad_middle_part
    branch_grad = grad_middle.astype(BF16)
    branch_all = both(branch_grad)

    up_power = jnp.maximum(power_for(normed_two_all, grad_pre), power_for(branch_all, attn_mixed))
    up_scale = jnp.exp2(-up_power)
    grad_up = (tn(normed_two_all, grad_pre) * up_scale).astype(F16)
    grad_out_w = (tn(branch_all, attn_mixed) * up_scale).astype(F16)
    grad_mid_t = ring.reduce(jnp.concatenate([grad_up, grad_out_w], axis=1), up_power)

    mlp_part = nt(hidden, down_t)
    mlp_local = mlp_part[:own] + other_core(mlp_part[own:].astype(BF16)).astype(F32)
    outputs = middle + (mlp_local + down_bias)

    grad_mixed = nn(branch_all, out_t).astype(BF16)
    grad_q, grad_k, grad_v = attend_backward(*stacked, score_scale, log_norm, grad_mixed.reshape(head_shape))
    grad_proj = jnp.concatenate([g.reshape(all_rows, half_width) for g in (grad_q, grad_k, grad_v)], axis=1).astype(BF16)
    one_power = power_for(normed_one, grad_proj)
    grad_one = (tn(normed_one, grad_proj) * jnp.exp2(-one_power)).astype(F16)
    grad_one_t = ring.reduce(grad_one, one_power)
    grad_one_part = nt(grad_proj, qkv_full)
    grad_normed_one = grad_one_part[:own] + other_core(grad_one_part[own:].astype(BF16)).astype(F32)
    first_pull = jax.vjp(norm_layer, inputs_wide, norm_gain[0], norm_bias[0])[1]
    grad_inputs_part, grad_gain_one, grad_shift_one = first_pull(grad_normed_one)
    grad_inputs = grad_middle + grad_inputs_part

    up_term = jnp.sum(grad_pre.astype(F32), axis=0)
    shared = jnp.concatenate(
        [
            grad_gain_two,
            grad_shift_two,
            jnp.sum(branch_grad.astype(F32), axis=0),
            jnp.sum(grad_out.astype(F32), axis=0),
        ]
    )
    early = ring.total(jnp.concatenate([shared + other_core(shared), up_term]))
    proj_wide = grad_proj.astype(F32)
    qv_term = jnp.concatenate([jnp.sum(proj_wide[:, :half_width], axis=0), jnp.sum(proj_wide[:, 2 * half_width :], axis=0)])
    shared_one = jnp.concatenate([grad_gain_one, grad_shift_one])
    late = ring.total(jnp.concatenate([shared_one + other_core(shared_one), qv_term]))

    cut = w_up.shape[1]
    grad_qkv_shard = jnp.stack([grad_one_t[:, k * half_width : (k + 1) * half_width] for k in range(3)])
    return (
        outputs,
        grad_inputs,
        jnp.stack([late[:width], early[:width]]),
        jnp.stack([late[width : 2 * width], early[width : 2 * width]]),
        grad_qkv_shard,
        late[2 * width :].reshape(2, half_width),
        grad_mid_t[:, cut:].T,
        early[2 * width : 3 * width],
        grad_mid_t[:, :cut],
        early[4 * width :],
        grad_down_t.T,
        early[3 * width : 4 * width],
    )


def solution(mesh):
    rows = P(("dp", "tensor"), None)
    return jax.shard_map(
        body,
        mesh=mesh,
        in_specs=(
            rows,
            P("dp", None),
            P(),
            P(),
            P(None, "dp", "tensor"),
            P(None, "tensor"),
            P("tensor", "dp"),
            P(),
            P("dp", "tensor"),
            P("tensor"),
            P("tensor", "dp"),
            P(),
            rows,
        ),
        out_specs=(
            rows,
            rows,
            P(),
            P(),
            P(None, "dp", "tensor"),
            P(None, "tensor"),
            P("tensor", "dp"),
            P(),
            P("dp", "tensor"),
            P("tensor"),
            P("tensor", "dp"),
            P(),
        ),
        check_vma=False,
    )
```
